32 devices in a mesh: shot: 8 (over y, x, core), depth: 4 (over z).
Axes of the slice: x: 2, y: 2, z: 4, core: 2. Of those that a mesh axis runs over, the one named last changes fastest.
Arguments:
- probes: bfloat16 [8, 64, 128, 128], P('shot', None, 'depth'), may hold values from -6 to 6
- courant: float32 [128, 128], P('depth'), may hold values from 0.1 to 0.45
- sketches: float32 [8, 128, 64], replicated, may hold values from -0.5 to 0.5
Outputs:
- basis: float32 [64, 128, 128], P(None, 'depth')
- cores: float32 [8, 64, 64], P('shot')
The draws below stay inside these ranges and needn't reach their ends.
All inputs are finite; a program needn't handle non-finite values.
Results may differ from the reference program's by a relative error of at most 0.0003.
Values may be sent and summed in bfloat16 or wider, within the bound.
A program may use at most 64 MiB of HBM per device.

```python
import math
import jax
import jax.numpy as jnp
from jax import lax

R = 64
NX = 128
STEPS = 4
SHOTS = 8
NZ = 128


def draw_probes(key, part):
    key_shot = jax.random.fold_in(key, 11)
    key_probe = jax.random.fold_in(key, 23)
    key_single = jax.random.fold_in(key, 37)
    per_shot = jax.random.normal(key_shot, (SHOTS, 1, NZ, NX), jnp.float32)
    per_probe = jax.random.normal(key_probe, (1, R, NZ, NX), jnp.float32)
    single = jax.random.normal(key_single, (SHOTS, R, NZ, NX), jnp.float32)
    mixture = 0.35 * per_shot + 0.45 * per_probe + 0.8216 * single
    return jnp.clip(mixture, -6.0, 6.0).astype(jnp.bfloat16)


def shard_levels(key, dims, pieces, low, top_value):
    level, own = 1.0, jax.random.fold_in(key, 6)
    for dim, shards_of in pieces:
        steps = jnp.exp(jax.random.uniform(jax.random.fold_in(own, dim), (shards_of,), jnp.float32, low / len(pieces), top_value / len(pieces)))
        level = level * jnp.repeat(steps, dims[dim] // shards_of).reshape([-1 if axis == dim else 1 for axis in range(len(dims))])
    return level


def gaussian(rng, shape, spread, bound, dtype=jnp.bfloat16):
    result = jax.random.normal(rng, shape, jnp.float32) * spread
    return jnp.minimum(jnp.maximum(result, -bound), bound).astype(dtype)


def setup_inputs(seed: int = 0) -> dict:
    seeds = jax.random.split(jax.random.key(seed), 4)
    probes = draw_probes(jax.random.fold_in(seeds[3], 71), 0)
    courant = jnp.clip(0.1 + 0.35 * jax.random.uniform(seeds[1], (NZ, NX), jnp.float32) ** shard_levels(seeds[1], (NZ, NX), ((0, 4),), -0.2, 0.2), 0.1, 0.45)
    sketches = gaussian(seeds[2], (SHOTS, 2 * R, R), (2 * R) ** -0.5, 0.5, jnp.float32)
    return dict(probes=probes, courant=courant, sketches=sketches)


def propagate(field, courant):
    earlier = field
    current = field
    for repeat in range(STEPS):
        padded = jnp.pad(current, ((0, 0), (1, 1), (1, 1)))
        laplace = padded[:, 2:, 1:-1] + padded[:, :-2, 1:-1] + padded[:, 1:-1, 2:] + padded[:, 1:-1, :-2] - 4.0 * current
        earlier, current = (current, 2.0 * current - earlier + courant * laplace)
    return current

def orthonormal(matrix):
    gram = jnp.dot(matrix, matrix.T, precision=lax.Precision.HIGHEST)
    lower_factor = jnp.linalg.cholesky(gram)
    return lax.linalg.triangular_solve(lower_factor, matrix, left_side=True, lower=True)

def response(probes, courant, shot_index):
    field = propagate(probes[shot_index].astype(jnp.float32), courant)
    return field.reshape(R, NZ * NX)

def merge_range(probes, courant, sketches, begin_at, end_at):
    if end_at - begin_at == 1:
        return orthonormal(response(probes, courant, begin_at))
    middle = (begin_at + end_at) // 2
    low_factor = merge_range(probes, courant, sketches, begin_at, middle)
    high_factor = merge_range(probes, courant, sketches, middle, end_at)
    sketch = sketches[middle - 1]
    mixed = jnp.dot(sketch[:R].T, low_factor, precision=lax.Precision.HIGHEST) + jnp.dot(sketch[R:].T, high_factor, precision=lax.Precision.HIGHEST)
    return orthonormal(mixed)

def reference(probes, courant, sketches):
    root = merge_range(probes, courant, sketches, 0, SHOTS)

    def project(shot_probes):
        field = propagate(shot_probes.astype(jnp.float32), courant).reshape(R, NZ * NX)
        return jnp.dot(root, field.T, precision=lax.Precision.HIGHEST) / math.sqrt(R)
    cores = lax.map(project, probes)
    return (root.reshape(R, NZ, NX), cores)
```

```python
import functools
import math

import jax
import jax.numpy as jnp
from jax import lax
from jax.experimental import pallas as pl
from jax.experimental.pallas import tpu as pltpu
from jax.sharding import PartitionSpec as P

STEPS = 4
MESH = pl.DeviceIdType.MESH
HI = lax.Precision.HIGHEST
NN = (((1,), (0,)), ((), ()))
NT = (((1,), (1,)), ((), ()))
TN = (((0,), (0,)), ((), ()))
PIECES = 4


def mm(a, b, dims=NN):
    return lax.dot_general(a, b, dims, precision=HI, preferred_element_type=jnp.float32)


def inverse_factor(gram):
    n = gram.shape[0]
    rows = lax.broadcasted_iota(jnp.int32, (n, 1), 0)
    eye = (
        lax.broadcasted_iota(jnp.int32, (n, n), 0) == lax.broadcasted_iota(jnp.int32, (n, n), 1)
    ).astype(jnp.float32)
    a = jnp.concatenate([gram, eye], axis=1)
    blocks = [a[8 * b : 8 * b + 8] for b in range(n // 8)]
    for k in range(n - 1):
        b0, r = divmod(k, 8)
        row = blocks[b0][r : r + 1]
        row = row * (1.0 / row[:, k : k + 1])
        for b in range((k + 1) // 8, n // 8):
            col = blocks[b][:, k : k + 1]
            if b == b0:
                col = jnp.where(rows[:8] > r, col, 0.0)
            blocks[b] = blocks[b] - col * row
    a = jnp.concatenate(blocks, axis=0)
    pivots = jnp.sum(a[:, :n] * eye, axis=1, keepdims=True)
    return a[:, n:] * (1.0 / jnp.sqrt(pivots))


def kernel(
    depths,
    levels,
    probes,
    speed,
    sketches,
    basis,
    cores,
    halo,
    wide_speed,
    field_a,
    field_b,
    pairs,
    sums,
    sums_in,
    halo_send,
    halo_recv,
    speed_send,
    speed_recv,
    pair_send,
    pair_recv,
    fwd_send,
    fwd_recv,
    sum_send,
    sum_recv,
):
    rows, rank, cells = probes.shape
    shot = lax.axis_index("shot")
    depth = lax.axis_index("depth")
    low_end = depth == 0
    high_end = depth == depths - 1

    def bit(h):
        return lax.rem(shot // (2**h), 2)

    def peer(h):
        return shot + 2**h - 2 ** (h + 1) * bit(h)

    barrier = pltpu.get_barrier_semaphore()
    for h in range(levels):
        pl.semaphore_signal(barrier, inc=1, device_id=(peer(h), depth), device_id_type=MESH)
    for j in range(1, depths):
        other = lax.rem(depth + j, depths)
        pl.semaphore_signal(barrier, inc=1, device_id=(shot, other), device_id_type=MESH)
    pl.semaphore_wait(barrier, levels + depths - 1)

    def halo_copies(side):
        to = depth + 1 if side == 0 else depth - 1
        rows_out = pl.ds(rows - STEPS, STEPS) if side == 0 else pl.ds(0, STEPS)
        first = pltpu.make_async_remote_copy(
            src_ref=probes.at[rows_out],
            dst_ref=halo.at[side],
            send_sem=halo_send.at[side],
            recv_sem=halo_recv.at[side],
            device_id=(shot, to),
            device_id_type=MESH,
        )
        at = 0 if side == 0 else STEPS + rows
        second = pltpu.make_async_remote_copy(
            src_ref=speed.at[rows_out],
            dst_ref=wide_speed.at[pl.ds(at, STEPS)],
            send_sem=speed_send.at[side],
            recv_sem=speed_recv.at[side],
            device_id=(shot, to),
            device_id_type=MESH,
        )
        return first, second

    @pl.when(depth < depths - 1)
    def _():
        for c in halo_copies(0):
            c.start()

    @pl.when(depth > 0)
    def _():
        for c in halo_copies(1):
            c.start()

    @pl.loop(0, rows)
    def _(d):
        field_a[STEPS + d] = probes[d].astype(jnp.float32)

    wide_speed[STEPS : STEPS + rows] = speed[...]

    @pl.when(depth > 0)
    def _():
        for c in halo_copies(0):
            c.wait_recv()
        field_a[0:STEPS] = halo[0].astype(jnp.float32)

    @pl.when(depth == 0)
    def _():
        field_a[0:STEPS] = jnp.zeros((STEPS, rank, cells), jnp.float32)
        wide_speed[0:STEPS] = jnp.zeros((STEPS, cells), jnp.float32)

    @pl.when(depth < depths - 1)
    def _():
        for c in halo_copies(1):
            c.wait_recv()
        field_a[STEPS + rows : 2 * STEPS + rows] = halo[1].astype(jnp.float32)

    @pl.when(depth == depths - 1)
    def _():
        field_a[STEPS + rows : 2 * STEPS + rows] = jnp.zeros((STEPS, rank, cells), jnp.float32)
        wide_speed[STEPS + rows : 2 * STEPS + rows] = jnp.zeros((STEPS, cells), jnp.float32)

    lane = lax.broadcasted_iota(jnp.int32, (rank, cells), 1)
    not_first = lane > 0
    not_last = lane < cells - 1
    me = bit(0)
    mine = pl.ds(pl.multiple_of(me * rank, rank), rank)

    def update(d, source, older):
        u = source[d]
        left = jnp.where(not_first, pltpu.roll(u, 1, 1), 0.0)
        right = jnp.where(not_last, pltpu.roll(u, cells - 1, 1), 0.0)
        laplace = source[d + 1] + source[d - 1] + right + left - 4.0 * u
        return 2.0 * u - older + wide_speed[pl.ds(d, 1)] * laplace

    for step in range(STEPS):
        source, target = (field_a, field_b) if step % 2 == 0 else (field_b, field_a)
        last = step == STEPS - 1

        @pl.loop(step + 1, 2 * STEPS + rows - step - 1)
        def _(d):
            older = source[d] if step == 0 else target[d]
            new = update(d, source, older)
            if last:
                pairs[0, d - STEPS, mine] = new
            else:
                target[d] = new

    def pair_copy(h):
        own = pl.ds(pl.multiple_of(bit(h) * rank, rank), rank)
        return [
            pltpu.make_async_remote_copy(
                src_ref=pairs.at[h, :, own],
                dst_ref=pairs.at[h, :, own],
                send_sem=pair_send.at[h, 0],
                recv_sem=pair_recv.at[h, 0],
                device_id=(peer(h), depth),
                device_id_type=MESH,
            )
        ]

    for c in pair_copy(0):
        c.start()
    for c in pair_copy(0):
        c.wait()

    def gram_body(d, total):
        x = pairs[0, d]
        return total + mm(x, x, NT)

    zero = jnp.zeros((2 * rank, 2 * rank), jnp.float32)
    gram = lax.fori_loop(0, rows, gram_body, zero)

    def sum_copy(h, j):
        other = lax.rem(depth + j, depths)
        size = 2 * rank if h == 0 else rank
        return pltpu.make_async_remote_copy(
            src_ref=sums.at[h, pl.ds(0, size)],
            dst_ref=sums_in.at[h, depth, pl.ds(0, size)],
            send_sem=sum_send.at[h, j],
            recv_sem=sum_recv.at[h, j],
            device_id=(shot, other),
            device_id_type=MESH,
        )

    def depth_sum(h, value):
        size = value.shape[0]
        sums[h, 0:size] = value
        for j in range(1, depths):
            sum_copy(h, j).start()
        for j in range(1, depths):
            sum_copy(h, j).wait()
        total = None
        for j in range(depths):
            part = jnp.where(depth == j, value, sums_in[h, j, 0:size])
            total = part if total is None else total + part
        return total

    for h in range(levels):
        sums_in[h, depth] = jnp.zeros((2 * rank, 2 * rank), jnp.float32)
    gram = depth_sum(0, gram)

    low = inverse_factor(gram[:rank, :rank])
    high = inverse_factor(gram[rank:, rank:])
    sketch = sketches[shot // 2 * 2]
    mixer = jnp.concatenate(
        [mm(sketch[:rank], low, TN), mm(sketch[rank:], high, TN)], axis=1
    )
    carried = mm(mixer, gram)
    inverse = inverse_factor(mm(carried, mixer, NT))
    mixer = mm(inverse, mixer)
    carried = mm(inverse, carried)
    projected = jnp.where(me == 0, carried[:, :rank], carried[:, rank:])

    for h in range(1, levels):
        own_bit = bit(h)
        own = pl.ds(pl.multiple_of(own_bit * rank, rank), rank)

        @pl.loop(0, rows)
        def _(d):
            pairs[h, d, own] = mm(mixer, pairs[h - 1, d])

        per = rows // 2 // PIECES
        half = rows // 2

        def piece_copy(i):
            at = pl.ds(me * half + i * per, per)
            return pltpu.make_async_remote_copy(
                src_ref=pairs.at[h, at, own],
                dst_ref=pairs.at[h, at, own],
                send_sem=pair_send.at[h, i],
                recv_sem=pair_recv.at[h, i],
                device_id=(peer(h), depth),
                device_id_type=MESH,
            )

        got = pl.ds(pl.multiple_of((1 - own_bit) * rank, rank), rank)

        def forward_copy(i):
            at = pl.ds(me * half + i * per, per)
            return pltpu.make_async_remote_copy(
                src_ref=pairs.at[h, at, got],
                dst_ref=pairs.at[h, at, got],
                send_sem=fwd_send.at[h, i],
                recv_sem=fwd_recv.at[h, i],
                device_id=(peer(0), depth),
                device_id_type=MESH,
            )

        for i in range(PIECES):
            piece_copy(i).start()
        for i in range(PIECES):
            piece_copy(i).wait_recv()
            forward_copy(i).start()
        for i in range(PIECES):
            piece_copy(i).wait_send()
            forward_copy(i).wait()

        def cross_body(d, total):
            y = pairs[h, d]
            r = pairs[0, d, mine]
            return total + mm(y, jnp.concatenate([y[rank:], r], axis=0), NT)

        cross = lax.fori_loop(0, rows, cross_body, zero)
        value = jnp.concatenate(
            [
                cross[:rank, :rank],
                jnp.where(own_bit == 0, cross[rank:, rank:], cross[:rank, rank:]),
            ],
            axis=1,
        )
        value = depth_sum(h, value)
        stride = 2**h
        sketch = sketches[shot // (2 * stride) * (2 * stride) + stride - 1]
        top, bottom = sketch[:rank], sketch[rank:]
        across = value[:, :rank]
        mixed = mm(sketch, sketch, TN)
        mixed += mm(top, mm(across, bottom), TN) + mm(bottom, mm(across, top, TN), TN)
        inverse = inverse_factor(mixed)
        mixer = mm(inverse, sketch, NT)
        other = value[:, rank:]
        low_part = jnp.where(own_bit == 0, projected, other)
        high_part = jnp.where(own_bit == 0, other, projected)
        projected = mm(mixer, jnp.concatenate([low_part, high_part], axis=0))

    @pl.loop(0, rows)
    def _(d):
        basis[d] = mm(mixer, pairs[levels - 1, d])

    cores[...] = projected * (1.0 / math.sqrt(rank))

    @pl.when(depth < depths - 1)
    def _():
        for c in halo_copies(0):
            c.wait_send()

    @pl.when(depth > 0)
    def _():
        for c in halo_copies(1):
            c.wait_send()


def body(probes, courant, sketches):
    depths = lax.axis_size("depth")
    levels = lax.axis_size("shot").bit_length() - 1
    local = jnp.transpose(probes[0], (1, 0, 2))
    rows, rank, cells = local.shape
    f32 = jnp.float32
    vmem = pl.BlockSpec(memory_space=pltpu.VMEM)
    dma = pltpu.SemaphoreType.DMA
    basis, cores = pl.pallas_call(
        functools.partial(kernel, depths, levels),
        out_shape=(
            jax.ShapeDtypeStruct((rows, rank, cells), f32),
            jax.ShapeDtypeStruct((rank, rank), f32),
        ),
        in_specs=[vmem] * 3,
        out_specs=(vmem, vmem),
        scratch_shapes=[
            pltpu.VMEM((2, STEPS, rank, cells), jnp.bfloat16),
            pltpu.VMEM((rows + 2 * STEPS, cells), f32),
            pltpu.VMEM((rows + 2 * STEPS, rank, cells), f32),
            pltpu.VMEM((rows + 2 * STEPS, rank, cells), f32),
            pltpu.VMEM((levels, rows, 2 * rank, cells), f32),
            pltpu.VMEM((levels, 2 * rank, 2 * rank), f32),
            pltpu.VMEM((levels, depths, 2 * rank, 2 * rank), f32),
            dma((2,)),
            dma((2,)),
            dma((2,)),
            dma((2,)),
            dma((levels, PIECES)),
            dma((levels, PIECES)),
            dma((levels, PIECES)),
            dma((levels, PIECES)),
            dma((levels, depths)),
            dma((levels, depths)),
        ],
        compiler_params=pltpu.CompilerParams(
            collective_id=0, has_side_effects=True, vmem_limit_bytes=56 * 2**20
        ),
    )(local, courant, sketches)
    return (jnp.transpose(basis, (1, 0, 2)), cores[None])


def solution(mesh):
    placed = (P("shot", None, "depth", None), P("depth", None), P())
    return jax.shard_map(
        body,
        mesh=mesh,
        in_specs=placed,
        out_specs=(P(None, "depth", None), P("shot", None, None)),
        check_vma=False,
    )
```

```python
import functools
import math

import jax
import jax.numpy as jnp
from jax import lax
from jax.experimental import pallas as pl
from jax.experimental.pallas import tpu as pltpu
from jax.sharding import PartitionSpec as P

STEPS = 4
MESH = pl.DeviceIdType.MESH
HI = lax.Precision.HIGHEST
NN = (((1,), (0,)), ((), ()))
NT = (((1,), (1,)), ((), ()))
TN = (((0,), (0,)), ((), ()))
PIECES = 4
WIDTH = 8


def mm(a, b, dims=NN):
    return lax.dot_general(a, b, dims, precision=HI, preferred_element_type=jnp.float32)


def split(x):
    top = x.astype(jnp.bfloat16)
    return top, (x - top.astype(jnp.float32)).astype(jnp.bfloat16)


def mm3(a, b, dims=NN):
    def part(p, q):
        return lax.dot_general(p, q, dims, preferred_element_type=jnp.float32)

    return part(a[0], b[0]) + (part(a[0], b[1]) + part(a[1], b[0]))


def wide(ref, h, d, picked=slice(None)):
    return jnp.concatenate([ref[h, d + i, picked] for i in range(WIDTH)], axis=1)


def inverse_factor(gram):
    n = gram.shape[0]
    rows = lax.broadcasted_iota(jnp.int32, (n, 1), 0)
    eye = (
        lax.broadcasted_iota(jnp.int32, (n, n), 0) == lax.broadcasted_iota(jnp.int32, (n, n), 1)
    ).astype(jnp.float32)
    a = jnp.concatenate([gram, eye], axis=1)
    blocks = [a[8 * b : 8 * b + 8] for b in range(n // 8)]
    for k in range(0, n, 2):
        b0, r = divmod(k, 8)
        first, second = blocks[b0][r : r + 1], blocks[b0][r + 1 : r + 2]
        p, q, s = first[:, k : k + 1], second[:, k : k + 1], second[:, k + 1 : k + 2]
        if k == n - 2:
            break
        scale = 1.0 / (p * s - q * q)
        row0 = (s * first - q * second) * scale
        row1 = (p * second - q * first) * scale
        for b in range((k + 2) // 8, n // 8):
            col0, col1 = blocks[b][:, k : k + 1], blocks[b][:, k + 1 : k + 2]
            if b == b0:
                below = rows[:8] > r + 1
                col0, col1 = jnp.where(below, col0, 0.0), jnp.where(below, col1, 0.0)
            blocks[b] = blocks[b] - (col0 * row0 + col1 * row1)
    a = jnp.concatenate(blocks, axis=0)
    before = jnp.concatenate([a[n - 1 :], a[: n - 1]], axis=0)
    even = lax.rem(rows, 2) == 0
    own = jnp.sum(a[:, :n] * eye, axis=1, keepdims=True)
    shifted = jnp.concatenate([eye[n - 1 :], eye[: n - 1]], axis=0)
    side = jnp.sum(a[:, :n] * shifted, axis=1, keepdims=True)
    above = jnp.sum(before[:, :n] * shifted, axis=1, keepdims=True)
    ratio = jnp.where(even, 0.0, side / jnp.where(even, 1.0, above))
    value = own - ratio * side
    return (a[:, n:] - ratio * before[:, n:]) * (1.0 / jnp.sqrt(value))


def kernel(
    depths,
    levels,
    probes,
    speed,
    sketches,
    basis,
    cores,
    halo,
    wide_speed,
    field_a,
    field_b,
    pairs,
    sums,
    sums_in,
    halo_send,
    halo_recv,
    speed_send,
    speed_recv,
    pair_send,
    pair_recv,
    fwd_send,
    fwd_recv,
    sum_send,
    sum_recv,
):
    rows, rank, cells = probes.shape
    shot = lax.axis_index("shot")
    depth = lax.axis_index("depth")
    low_end = depth == 0
    high_end = depth == depths - 1

    def bit(h):
        return lax.rem(shot // (2**h), 2)

    def peer(h):
        return shot + 2**h - 2 ** (h + 1) * bit(h)

    barrier = pltpu.get_barrier_semaphore()
    for h in range(levels):
        pl.semaphore_signal(barrier, inc=1, device_id=(peer(h), depth), device_id_type=MESH)
    for j in range(1, depths):
        other = lax.rem(depth + j, depths)
        pl.semaphore_signal(barrier, inc=1, device_id=(shot, other), device_id_type=MESH)
    pl.semaphore_wait(barrier, levels + depths - 1)

    def halo_copies(side):
        to = depth + 1 if side == 0 else depth - 1
        rows_out = pl.ds(rows - STEPS, STEPS) if side == 0 else pl.ds(0, STEPS)
        first = pltpu.make_async_remote_copy(
            src_ref=probes.at[rows_out],
            dst_ref=halo.at[side],
            send_sem=halo_send.at[side],
            recv_sem=halo_recv.at[side],
            device_id=(shot, to),
            device_id_type=MESH,
        )
        at = 0 if side == 0 else STEPS + rows
        second = pltpu.make_async_remote_copy(
            src_ref=speed.at[rows_out],
            dst_ref=wide_speed.at[pl.ds(at, STEPS)],
            send_sem=speed_send.at[side],
            recv_sem=speed_recv.at[side],
            device_id=(shot, to),
            device_id_type=MESH,
        )
        return first, second

    @pl.when(depth < depths - 1)
    def _():
        for c in halo_copies(0):
            c.start()

    @pl.when(depth > 0)
    def _():
        for c in halo_copies(1):
            c.start()

    @pl.loop(0, rows, unroll=4)
    def _(d):
        field_a[STEPS + d] = probes[d].astype(jnp.float32)

    wide_speed[STEPS : STEPS + rows] = speed[...]

    @pl.when(depth > 0)
    def _():
        for c in halo_copies(0):
            c.wait_recv()
        field_a[0:STEPS] = halo[0].astype(jnp.float32)

    @pl.when(depth == 0)
    def _():
        field_a[0:STEPS] = jnp.zeros((STEPS, rank, cells), jnp.float32)
        wide_speed[0:STEPS] = jnp.zeros((STEPS, cells), jnp.float32)

    @pl.when(depth < depths - 1)
    def _():
        for c in halo_copies(1):
            c.wait_recv()
        field_a[STEPS + rows : 2 * STEPS + rows] = halo[1].astype(jnp.float32)

    @pl.when(depth == depths - 1)
    def _():
        field_a[STEPS + rows : 2 * STEPS + rows] = jnp.zeros((STEPS, rank, cells), jnp.float32)
        wide_speed[STEPS + rows : 2 * STEPS + rows] = jnp.zeros((STEPS, cells), jnp.float32)

    lane = lax.broadcasted_iota(jnp.int32, (rank, cells), 1)
    not_first = lane > 0
    not_last = lane < cells - 1
    me = bit(0)
    mine = pl.ds(pl.multiple_of(me * rank, rank), rank)

    def update(d, source, older):
        u = source[d]
        left = jnp.where(not_first, pltpu.roll(u, 1, 1), 0.0)
        right = jnp.where(not_last, pltpu.roll(u, cells - 1, 1), 0.0)
        laplace = source[d + 1] + source[d - 1] + right + left - 4.0 * u
        return 2.0 * u - older + wide_speed[pl.ds(d, 1)] * laplace

    for step in range(STEPS):
        source, target = (field_a, field_b) if step % 2 == 0 else (field_b, field_a)
        last = step == STEPS - 1

        @pl.loop(step + 1, 2 * STEPS + rows - step - 1, unroll=2)
        def _(d):
            older = source[d] if step == 0 else target[d]
            new = update(d, source, older)
            if last:
                pairs[0, d - STEPS, mine] = new
            else:
                target[d] = new

    def pair_copy(h):
        own = pl.ds(pl.multiple_of(bit(h) * rank, rank), rank)
        return [
            pltpu.make_async_remote_copy(
                src_ref=pairs.at[h, :, own],
                dst_ref=pairs.at[h, :, own],
                send_sem=pair_send.at[h, 0],
                recv_sem=pair_recv.at[h, 0],
                device_id=(peer(h), depth),
                device_id_type=MESH,
            )
        ]

    for c in pair_copy(0):
        c.start()
    for c in pair_copy(0):
        c.wait()

    def gram_body(d, total):
        x = split(wide(pairs, 0, d * WIDTH))
        return total + mm3(x, x, NT)

    zero = jnp.zeros((2 * rank, 2 * rank), jnp.float32)
    gram = lax.fori_loop(0, rows // WIDTH, gram_body, zero)

    def sum_copy(h, j):
        other = lax.rem(depth + j, depths)
        size = 2 * rank if h == 0 else rank
        return pltpu.make_async_remote_copy(
            src_ref=sums.at[h, pl.ds(0, size)],
            dst_ref=sums_in.at[h, depth, pl.ds(0, size)],
            send_sem=sum_send.at[h, j],
            recv_sem=sum_recv.at[h, j],
            device_id=(shot, other),
            device_id_type=MESH,
        )

    def depth_sum(h, value):
        size = value.shape[0]
        sums[h, 0:size] = value
        for j in range(1, depths):
            sum_copy(h, j).start()
        for j in range(1, depths):
            sum_copy(h, j).wait()
        total = None
        for j in range(depths):
            part = jnp.where(depth == j, value, sums_in[h, j, 0:size])
            total = part if total is None else total + part
        return total

    for h in range(levels):
        sums_in[h, depth] = jnp.zeros((2 * rank, 2 * rank), jnp.float32)
    gram = depth_sum(0, gram)

    low = inverse_factor(gram[:rank, :rank])
    high = inverse_factor(gram[rank:, rank:])
    sketch = sketches[shot // 2 * 2]
    mixer = jnp.concatenate(
        [mm(sketch[:rank], low, TN), mm(sketch[rank:], high, TN)], axis=1
    )
    carried = mm(mixer, gram)
    inverse = inverse_factor(mm(carried, mixer, NT))
    mixer = mm(inverse, mixer)
    carried = mm(inverse, carried)
    projected = jnp.where(me == 0, carried[:, :rank], carried[:, rank:])

    for h in range(1, levels):
        own_bit = bit(h)
        own = pl.ds(pl.multiple_of(own_bit * rank, rank), rank)

        parts = split(mixer)

        @pl.loop(0, rows // WIDTH)
        def _(i):
            out = mm3(parts, split(wide(pairs, h - 1, i * WIDTH)))
            for w in range(WIDTH):
                pairs[h, i * WIDTH + w, own] = out[:, w * cells : (w + 1) * cells]

        per = rows // 2 // PIECES
        half = rows // 2

        def piece_copy(i):
            at = pl.ds(me * half + i * per, per)
            return pltpu.make_async_remote_copy(
                src_ref=pairs.at[h, at, own],
                dst_ref=pairs.at[h, at, own],
                send_sem=pair_send.at[h, i],
                recv_sem=pair_recv.at[h, i],
                device_id=(peer(h), depth),
                device_id_type=MESH,
            )

        got = pl.ds(pl.multiple_of((1 - own_bit) * rank, rank), rank)

        def forward_copy(i):
            at = pl.ds(me * half + i * per, per)
            return pltpu.make_async_remote_copy(
                src_ref=pairs.at[h, at, got],
                dst_ref=pairs.at[h, at, got],
                send_sem=fwd_send.at[h, i],
                recv_sem=fwd_recv.at[h, i],
                device_id=(peer(0), depth),
                device_id_type=MESH,
            )

        for i in range(PIECES):
            piece_copy(i).start()
        for i in range(PIECES):
            piece_copy(i).wait_recv()
            forward_copy(i).start()
        for i in range(PIECES):
            piece_copy(i).wait_send()
            forward_copy(i).wait()

        def cross_body(d, total):
            y = split(wide(pairs, h, d * WIDTH))
            r = split(wide(pairs, 0, d * WIDTH, mine))
            right = [jnp.concatenate([p[rank:], q], axis=0) for p, q in zip(y, r)]
            return total + mm3(y, right, NT)

        cross = lax.fori_loop(0, rows // WIDTH, cross_body, zero)
        value = jnp.concatenate(
            [
                cross[:rank, :rank],
                jnp.where(own_bit == 0, cross[rank:, rank:], cross[:rank, rank:]),
            ],
            axis=1,
        )
        value = depth_sum(h, value)
        stride = 2**h
        sketch = sketches[shot // (2 * stride) * (2 * stride) + stride - 1]
        top, bottom = sketch[:rank], sketch[rank:]
        across = value[:, :rank]
        mixed = mm(sketch, sketch, TN)
        mixed += mm(top, mm(across, bottom), TN) + mm(bottom, mm(across, top, TN), TN)
        inverse = inverse_factor(mixed)
        mixer = mm(inverse, sketch, NT)
        other = value[:, rank:]
        low_part = jnp.where(own_bit == 0, projected, other)
        high_part = jnp.where(own_bit == 0, other, projected)
        projected = mm(mixer, jnp.concatenate([low_part, high_part], axis=0))

    parts = split(mixer)

    @pl.loop(0, rows // WIDTH)
    def _(i):
        out = mm3(parts, split(wide(pairs, levels - 1, i * WIDTH)))
        for w in range(WIDTH):
            basis[i * WIDTH + w] = out[:, w * cells : (w + 1) * cells]

    cores[...] = projected * (1.0 / math.sqrt(rank))

    @pl.when(depth < depths - 1)
    def _():
        for c in halo_copies(0):
            c.wait_send()

    @pl.when(depth > 0)
    def _():
        for c in halo_copies(1):
            c.wait_send()


def body(probes, courant, sketches):
    depths = lax.axis_size("depth")
    levels = lax.axis_size("shot").bit_length() - 1
    local = jnp.transpose(probes[0], (1, 0, 2))
    rows, rank, cells = local.shape
    f32 = jnp.float32
    vmem = pl.BlockSpec(memory_space=pltpu.VMEM)
    dma = pltpu.SemaphoreType.DMA
    basis, cores = pl.pallas_call(
        functools.partial(kernel, depths, levels),
        out_shape=(
            jax.ShapeDtypeStruct((rows, rank, cells), f32),
            jax.ShapeDtypeStruct((rank, rank), f32),
        ),
        in_specs=[vmem] * 3,
        out_specs=(vmem, vmem),
        scratch_shapes=[
            pltpu.VMEM((2, STEPS, rank, cells), jnp.bfloat16),
            pltpu.VMEM((rows + 2 * STEPS, cells), f32),
            pltpu.VMEM((rows + 2 * STEPS, rank, cells), f32),
            pltpu.VMEM((rows + 2 * STEPS, rank, cells), f32),
            pltpu.VMEM((levels, rows, 2 * rank, cells), f32),
            pltpu.VMEM((levels, 2 * rank, 2 * rank), f32),
            pltpu.VMEM((levels, depths, 2 * rank, 2 * rank), f32),
            dma((2,)),
            dma((2,)),
            dma((2,)),
            dma((2,)),
            dma((levels, PIECES)),
            dma((levels, PIECES)),
            dma((levels, PIECES)),
            dma((levels, PIECES)),
            dma((levels, depths)),
            dma((levels, depths)),
        ],
        compiler_params=pltpu.CompilerParams(
            collective_id=0, has_side_effects=True, vmem_limit_bytes=56 * 2**20
        ),
    )(local, courant, sketches)
    return (jnp.transpose(basis, (1, 0, 2)), cores[None])


def solution(mesh):
    placed = (P("shot", None, "depth", None), P("depth", None), P())
    return jax.shard_map(
        body,
        mesh=mesh,
        in_specs=placed,
        out_specs=(P(None, "depth", None), P("shot", None, None)),
        check_vma=False,
    )
```

```python
import functools
import math

import jax
import jax.numpy as jnp
from jax import lax
from jax.experimental import pallas as pl
from jax.experimental.pallas import tpu as pltpu
from jax.sharding import PartitionSpec as P

STEPS = 4
MESH = pl.DeviceIdType.MESH
HI = lax.Precision.HIGHEST
NN = (((1,), (0,)), ((), ()))
NT = (((1,), (1,)), ((), ()))
TN = (((0,), (0,)), ((), ()))
PIECES = 2
WIDTH = 8


def mm(a, b, dims=NN):
    return lax.dot_general(a, b, dims, precision=HI, preferred_element_type=jnp.float32)


def split(x):
    top = x.astype(jnp.bfloat16)
    return top, (x - top.astype(jnp.float32)).astype(jnp.bfloat16)


def mm3(a, b, dims=NN):
    def part(p, q):
        return lax.dot_general(p, q, dims, preferred_element_type=jnp.float32)

    return part(a[0], b[0]) + (part(a[0], b[1]) + part(a[1], b[0]))


def wide(ref, h, d, picked=slice(None)):
    return jnp.concatenate([ref[h, d + i, picked] for i in range(WIDTH)], axis=1)


def inverse_factor(gram):
    n = gram.shape[0]
    rows = lax.broadcasted_iota(jnp.int32, (n, 1), 0)
    eye = (
        lax.broadcasted_iota(jnp.int32, (n, n), 0) == lax.broadcasted_iota(jnp.int32, (n, n), 1)
    ).astype(jnp.float32)
    a = jnp.concatenate([gram, eye], axis=1)
    blocks = [a[8 * b : 8 * b + 8] for b in range(n // 8)]
    for k in range(0, n, 2):
        b0, r = divmod(k, 8)
        first, second = blocks[b0][r : r + 1], blocks[b0][r + 1 : r + 2]
        p, q, s = first[:, k : k + 1], second[:, k : k + 1], second[:, k + 1 : k + 2]
        if k == n - 2:
            break
        scale = 1.0 / (p * s - q * q)
        row0 = (s * first - q * second) * scale
        row1 = (p * second - q * first) * scale
        for b in range((k + 2) // 8, n // 8):
            col0, col1 = blocks[b][:, k : k + 1], blocks[b][:, k + 1 : k + 2]
            if b == b0:
                below = rows[:8] > r + 1
                col0, col1 = jnp.where(below, col0, 0.0), jnp.where(below, col1, 0.0)
            blocks[b] = blocks[b] - (col0 * row0 + col1 * row1)
    a = jnp.concatenate(blocks, axis=0)
    before = jnp.concatenate([a[n - 1 :], a[: n - 1]], axis=0)
    even = lax.rem(rows, 2) == 0
    own = jnp.sum(a[:, :n] * eye, axis=1, keepdims=True)
    shifted = jnp.concatenate([eye[n - 1 :], eye[: n - 1]], axis=0)
    side = jnp.sum(a[:, :n] * shifted, axis=1, keepdims=True)
    above = jnp.sum(before[:, :n] * shifted, axis=1, keepdims=True)
    ratio = jnp.where(even, 0.0, side / jnp.where(even, 1.0, above))
    value = own - ratio * side
    return (a[:, n:] - ratio * before[:, n:]) * (1.0 / jnp.sqrt(value))


def kernel(
    depths,
    levels,
    probes,
    speed,
    sketches,
    basis,
    cores,
    halo,
    wide_speed,
    field_a,
    field_b,
    pairs,
    sums,
    sums_in,
    halo_send,
    halo_recv,
    speed_send,
    speed_recv,
    pair_send,
    pair_recv,
    sum_send,
    sum_recv,
):
    rows, rank, cells = probes.shape
    shot = lax.axis_index("shot")
    depth = lax.axis_index("depth")
    low_end = depth == 0
    high_end = depth == depths - 1

    def bit(h):
        return lax.rem(shot // (2**h), 2)

    def peer(h):
        return shot + 2**h - 2 ** (h + 1) * bit(h)

    barrier = pltpu.get_barrier_semaphore()
    for h in range(levels):
        pl.semaphore_signal(barrier, inc=1, device_id=(peer(h), depth), device_id_type=MESH)
    for j in range(1, depths):
        other = lax.rem(depth + j, depths)
        pl.semaphore_signal(barrier, inc=1, device_id=(shot, other), device_id_type=MESH)
    pl.semaphore_wait(barrier, levels + depths - 1)

    def halo_copies(side):
        to = depth + 1 if side == 0 else depth - 1
        rows_out = pl.ds(rows - STEPS, STEPS) if side == 0 else pl.ds(0, STEPS)
        first = pltpu.make_async_remote_copy(
            src_ref=probes.at[rows_out],
            dst_ref=halo.at[side],
            send_sem=halo_send.at[side],
            recv_sem=halo_recv.at[side],
            device_id=(shot, to),
            device_id_type=MESH,
        )
        at = 0 if side == 0 else STEPS + rows
        second = pltpu.make_async_remote_copy(
            src_ref=speed.at[rows_out],
            dst_ref=wide_speed.at[pl.ds(at, STEPS)],
            send_sem=speed_send.at[side],
            recv_sem=speed_recv.at[side],
            device_id=(shot, to),
            device_id_type=MESH,
        )
        return first, second

    @pl.when(depth < depths - 1)
    def _():
        for c in halo_copies(0):
            c.start()

    @pl.when(depth > 0)
    def _():
        for c in halo_copies(1):
            c.start()

    @pl.loop(0, rows, unroll=4)
    def _(d):
        field_a[STEPS + d] = probes[d].astype(jnp.float32)

    wide_speed[STEPS : STEPS + rows] = speed[...]

    @pl.when(depth > 0)
    def _():
        for c in halo_copies(0):
            c.wait_recv()
        field_a[0:STEPS] = halo[0].astype(jnp.float32)

    @pl.when(depth == 0)
    def _():
        field_a[0:STEPS] = jnp.zeros((STEPS, rank, cells), jnp.float32)
        wide_speed[0:STEPS] = jnp.zeros((STEPS, cells), jnp.float32)

    @pl.when(depth < depths - 1)
    def _():
        for c in halo_copies(1):
            c.wait_recv()
        field_a[STEPS + rows : 2 * STEPS + rows] = halo[1].astype(jnp.float32)

    @pl.when(depth == depths - 1)
    def _():
        field_a[STEPS + rows : 2 * STEPS + rows] = jnp.zeros((STEPS, rank, cells), jnp.float32)
        wide_speed[STEPS + rows : 2 * STEPS + rows] = jnp.zeros((STEPS, cells), jnp.float32)

    lane = lax.broadcasted_iota(jnp.int32, (rank, cells), 1)
    not_first = lane > 0
    not_last = lane < cells - 1
    me = bit(0)
    mine = pl.ds(pl.multiple_of(me * rank, rank), rank)

    def update(d, source, older):
        u = source[d]
        left = jnp.where(not_first, pltpu.roll(u, 1, 1), 0.0)
        right = jnp.where(not_last, pltpu.roll(u, cells - 1, 1), 0.0)
        laplace = source[d + 1] + source[d - 1] + right + left - 4.0 * u
        return 2.0 * u - older + wide_speed[pl.ds(d, 1)] * laplace

    for step in range(STEPS):
        source, target = (field_a, field_b) if step % 2 == 0 else (field_b, field_a)
        last = step == STEPS - 1

        @pl.loop(step + 1, 2 * STEPS + rows - step - 1, unroll=2)
        def _(d):
            older = source[d] if step == 0 else target[d]
            new = update(d, source, older)
            if last:
                pairs[0, d - STEPS, mine] = new
            else:
                target[d] = new

    def pair_copy(h):
        own = pl.ds(pl.multiple_of(bit(h) * rank, rank), rank)
        return [
            pltpu.make_async_remote_copy(
                src_ref=pairs.at[h, :, own],
                dst_ref=pairs.at[h, :, own],
                send_sem=pair_send.at[h, 0, 0],
                recv_sem=pair_recv.at[h, 0, 0],
                device_id=(peer(h), depth),
                device_id_type=MESH,
            )
        ]

    for c in pair_copy(0):
        c.start()
    for c in pair_copy(0):
        c.wait()

    def gram_body(d, total):
        x = split(wide(pairs, 0, d * WIDTH))
        return total + mm3(x, x, NT)

    zero = jnp.zeros((2 * rank, 2 * rank), jnp.float32)
    gram = lax.fori_loop(0, rows // WIDTH, gram_body, zero)

    def sum_copy(h, j):
        other = lax.rem(depth + j, depths)
        size = 2 * rank if h == 0 else rank
        return pltpu.make_async_remote_copy(
            src_ref=sums.at[h, pl.ds(0, size)],
            dst_ref=sums_in.at[h, depth, pl.ds(0, size)],
            send_sem=sum_send.at[h, j],
            recv_sem=sum_recv.at[h, j],
            device_id=(shot, other),
            device_id_type=MESH,
        )

    def depth_sum(h, value):
        size = value.shape[0]
        sums[h, 0:size] = value
        for j in range(1, depths):
            sum_copy(h, j).start()
        for j in range(1, depths):
            sum_copy(h, j).wait()
        total = None
        for j in range(depths):
            part = jnp.where(depth == j, value, sums_in[h, j, 0:size])
            total = part if total is None else total + part
        return total

    for h in range(levels):
        sums_in[h, depth] = jnp.zeros((2 * rank, 2 * rank), jnp.float32)
    gram = depth_sum(0, gram)

    low = inverse_factor(gram[:rank, :rank])
    high = inverse_factor(gram[rank:, rank:])
    sketch = sketches[shot // 2 * 2]
    mixer = jnp.concatenate(
        [mm(sketch[:rank], low, TN), mm(sketch[rank:], high, TN)], axis=1
    )
    carried = mm(mixer, gram)
    inverse = inverse_factor(mm(carried, mixer, NT))
    mixer = mm(inverse, mixer)
    carried = mm(inverse, carried)
    projected = jnp.where(me == 0, carried[:, :rank], carried[:, rank:])

    for h in range(1, levels):
        own_bit = bit(h)
        own = pl.ds(pl.multiple_of(own_bit * rank, rank), rank)

        parts = split(mixer)
        part_rows = rows // 2**h
        per = part_rows // PIECES
        got = pl.ds(pl.multiple_of((1 - own_bit) * rank, rank), rank)

        def part_at(mask, i):
            part = 0
            for b in range(h):
                part += 2**b * (1 - bit(b) if mask >> b & 1 else bit(b))
            return pl.ds(part * part_rows + i * per, per)

        def part_copy(mask, i):
            low = mask & -mask
            at = part_at(mask - low, i)
            lanes = got if mask else own
            return pltpu.make_async_remote_copy(
                src_ref=pairs.at[h, at, lanes],
                dst_ref=pairs.at[h, at, lanes],
                send_sem=pair_send.at[h, mask, i],
                recv_sem=pair_recv.at[h, mask, i],
                device_id=(peer(low.bit_length() - 1 if mask else h), depth),
                device_id_type=MESH,
            )

        chunks = rows // WIDTH
        ahead = max(1, part_rows // WIDTH)
        first = part_at(0, 0).start // WIDTH
        for t in range(chunks):
            at = lax.rem(first + t, chunks) * WIDTH
            out = mm3(parts, split(wide(pairs, h - 1, at)))
            for w in range(WIDTH):
                pairs[h, at + w, own] = out[:, w * cells : (w + 1) * cells]
            if per == WIDTH and t < PIECES:
                part_copy(0, t).start()
            elif per != WIDTH and t == ahead - 1:
                for i in range(PIECES):
                    part_copy(0, i).start()
        masks = sorted(range(2**h), key=lambda m: (m.bit_count(), -m))
        for mask in masks:
            low = mask & -mask if mask else 2**h
            for i in range(PIECES):
                part_copy(mask, i).wait_recv()
                for b in reversed(range(low.bit_length() - 1)):
                    part_copy(mask + 2**b, i).start()
        for mask in masks:
            for i in range(PIECES):
                part_copy(mask, i).wait_send()

        def cross_body(d, total):
            y = split(wide(pairs, h, d * WIDTH))
            r = split(wide(pairs, 0, d * WIDTH, mine))
            right = [jnp.concatenate([p[rank:], q], axis=0) for p, q in zip(y, r)]
            return total + mm3(y, right, NT)

        cross = lax.fori_loop(0, rows // WIDTH, cross_body, zero)
        value = jnp.concatenate(
            [
                cross[:rank, :rank],
                jnp.where(own_bit == 0, cross[rank:, rank:], cross[:rank, rank:]),
            ],
            axis=1,
        )
        value = depth_sum(h, value)
        stride = 2**h
        sketch = sketches[shot // (2 * stride) * (2 * stride) + stride - 1]
        top, bottom = sketch[:rank], sketch[rank:]
        across = value[:, :rank]
        mixed = mm(sketch, sketch, TN)
        mixed += mm(top, mm(across, bottom), TN) + mm(bottom, mm(across, top, TN), TN)
        inverse = inverse_factor(mixed)
        mixer = mm(inverse, sketch, NT)
        other = value[:, rank:]
        low_part = jnp.where(own_bit == 0, projected, other)
        high_part = jnp.where(own_bit == 0, other, projected)
        projected = mm(mixer, jnp.concatenate([low_part, high_part], axis=0))

    parts = split(mixer)

    @pl.loop(0, rows // WIDTH)
    def _(i):
        out = mm3(parts, split(wide(pairs, levels - 1, i * WIDTH)))
        for w in range(WIDTH):
            basis[i * WIDTH + w] = out[:, w * cells : (w + 1) * cells]

    cores[...] = projected * (1.0 / math.sqrt(rank))

    @pl.when(depth < depths - 1)
    def _():
        for c in halo_copies(0):
            c.wait_send()

    @pl.when(depth > 0)
    def _():
        for c in halo_copies(1):
            c.wait_send()


def body(probes, courant, sketches):
    depths = lax.axis_size("depth")
    levels = lax.axis_size("shot").bit_length() - 1
    local = jnp.transpose(probes[0], (1, 0, 2))
    rows, rank, cells = local.shape
    f32 = jnp.float32
    vmem = pl.BlockSpec(memory_space=pltpu.VMEM)
    dma = pltpu.SemaphoreType.DMA
    basis, cores = pl.pallas_call(
        functools.partial(kernel, depths, levels),
        out_shape=(
            jax.ShapeDtypeStruct((rows, rank, cells), f32),
            jax.ShapeDtypeStruct((rank, rank), f32),
        ),
        in_specs=[vmem] * 3,
        out_specs=(vmem, vmem),
        scratch_shapes=[
            pltpu.VMEM((2, STEPS, rank, cells), jnp.bfloat16),
            pltpu.VMEM((rows + 2 * STEPS, cells), f32),
            pltpu.VMEM((rows + 2 * STEPS, rank, cells), f32),
            pltpu.VMEM((rows + 2 * STEPS, rank, cells), f32),
            pltpu.VMEM((levels, rows, 2 * rank, cells), f32),
            pltpu.VMEM((levels, 2 * rank, 2 * rank), f32),
            pltpu.VMEM((levels, depths, 2 * rank, 2 * rank), f32),
            dma((2,)),
            dma((2,)),
            dma((2,)),
            dma((2,)),
            dma((levels, 2 ** (levels - 1), PIECES)),
            dma((levels, 2 ** (levels - 1), PIECES)),
            dma((levels, depths)),
            dma((levels, depths)),
        ],
        compiler_params=pltpu.CompilerParams(
            collective_id=0, has_side_effects=True, vmem_limit_bytes=56 * 2**20
        ),
    )(local, courant, sketches)
    return (jnp.transpose(basis, (1, 0, 2)), cores[None])


def solution(mesh):
    placed = (P("shot", None, "depth", None), P("depth", None), P())
    return jax.shard_map(
        body,
        mesh=mesh,
        in_specs=placed,
        out_specs=(P(None, "depth", None), P("shot", None, None)),
        check_vma=False,
    )
```
